256 devices in a mesh: mode: 16 (over x_hi, y, core), site: 16 (over z, x_lo).
Axes of the slice: x: 4 (x_hi: 2, x_lo: 2; x = x_hi * 2 + x_lo), y: 4, z: 8, core: 2. Of those that a mesh axis runs over, the one named last changes fastest.
Arguments:
- eigvecs: bfloat16 [2, 64, 3, 110592], P(None, 'mode', None, 'site'), may hold values from -6 to 6
- perams: bfloat16 [2, 16, 64, 64], replicated, may hold values from -0.75 to 0.75
- momenta: int32 [2, 3], replicated, may hold values from -2 to 2
- spins: int32 [16, 3], replicated, may hold values from 0 to 15
- pair_combs: int32 [16, 2], P('site'), may hold values from 0 to 15
- pair_moms: int32 [16, 2], P('site'), may hold values from 0 to 1
Outputs:
- exchange: float32 [16, 2, 64, 64], P('site', None, 'mode')
The draws below stay inside these ranges and needn't reach their ends.
All inputs are finite; a program needn't handle non-finite values.
Results may differ from the reference program's by a relative error of at most 0.018.
Values may be sent and summed in bfloat16 or wider, within the bound.
No kernel may reach another device: no remote copies, remote signals or barrier semaphores. Data moves between devices by JAX's collectives and lax.ppermute only.
A program may use at most 64 MiB of HBM per device.

```python
import jax
import jax.numpy as jnp
from jax import lax

NMODE = 64
LAT = 48
NSPIN = 16
COMB = 16
NMOM = 2
NSLICE = 2
SITES = 110592
PAIRS = 16


def touch_ends(drawn, stream_key, least, high):
    index_at = [jax.random.randint(jax.random.fold_in(stream_key, axis), (), 0, length) for axis, length in enumerate(drawn.shape)]
    longest = drawn.shape.index(max(drawn.shape))
    next_to = index_at[:longest] + [(index_at[longest] + 1) % drawn.shape[longest]] + index_at[longest + 1:]
    return drawn.at[tuple(index_at)].set(least).at[tuple(next_to)].set(high)


def block_scale(rng, extent, cuts, smallest, largest):
    loudness = 1.0
    for axis_at, shards_of in cuts:
        heights = jax.random.uniform(jax.random.fold_in(jax.random.fold_in(rng, 6), axis_at), (shards_of,), jnp.float32, smallest / len(cuts), largest / len(cuts))
        loudness = loudness * jnp.repeat(jnp.exp(heights), extent[axis_at] // shards_of).reshape((-1,) + (1,) * (len(extent) - 1 - axis_at))
    return loudness


def centred(key, extent, scale, reach, pieces=(), kind=jnp.bfloat16):
    loudness = block_scale(key, extent, pieces, -0.22, 0.18) if pieces else 1.0
    result = jax.random.normal(key, extent, jnp.float32) * scale * loudness
    return jnp.minimum(jnp.maximum(result, -reach), reach).astype(kind)


def setup_inputs(seed: int = 0) -> dict:
    streams_of = jax.random.split(jax.random.key(seed), 7)
    return {
        "eigvecs": centred(streams_of[0], (NSLICE, NMODE, 3, SITES), 1.0, 6.0, ((1, 16), (3, 16))),
        "perams": centred(streams_of[1], (NSLICE, NSPIN, NMODE, NMODE), NMODE ** -0.5, 0.75),
        "momenta": touch_ends(jax.random.randint(streams_of[2], (NMOM, 3), -2, 3), jax.random.fold_in(streams_of[2], 1), -2, 2).astype(jnp.int32),
        "spins": touch_ends(jax.random.randint(streams_of[3], (COMB, 3), 0, NSPIN), jax.random.fold_in(streams_of[3], 1), 0, NSPIN - 1).astype(jnp.int32),
        "pair_combs": touch_ends(jax.random.randint(streams_of[4], (PAIRS, 2), 0, COMB), jax.random.fold_in(streams_of[4], 1), 0, COMB - 1).astype(jnp.int32),
        "pair_moms": touch_ends(jax.random.randint(streams_of[5], (PAIRS, 2), 0, NMOM), jax.random.fold_in(streams_of[5], 1), 0, NMOM - 1).astype(jnp.int32),
    }


def hartley(momenta, glob):
    coord_x = glob // (LAT * LAT)
    coord_y = (glob // LAT) % LAT
    coord_z = glob % LAT
    wave = (momenta[:, 0:1] * coord_x[None] + momenta[:, 1:2] * coord_y[None] + momenta[:, 2:3] * coord_z[None]) % LAT
    theta = wave.astype(jnp.float32) * (2.0 * jnp.pi / LAT)
    return jnp.cos(theta) + jnp.sin(theta)


def triplet_slice(vectors, phase):
    floats = vectors.astype(jnp.float32)
    weighted = (phase[:, None, None, :] * floats[None]).astype(jnp.bfloat16).astype(jnp.float32)
    flat_w = weighted.reshape(NMOM * NMODE, 3 * SITES)

    def one_mode(index):
        left = floats[index]
        cross_0 = left[1][None] * floats[:, 2] - left[2][None] * floats[:, 1]
        cross_1 = left[2][None] * floats[:, 0] - left[0][None] * floats[:, 2]
        cross_2 = left[0][None] * floats[:, 1] - left[1][None] * floats[:, 0]
        diquark = jnp.stack([cross_0, cross_1, cross_2], axis=1).astype(jnp.bfloat16).astype(jnp.float32)
        return jnp.dot(diquark.reshape(NMODE, 3 * SITES), flat_w.T)

    summed = lax.map(one_mode, jnp.arange(NMODE))
    return (summed * (float(SITES) ** -0.5)).reshape(NMODE, NMODE, NMOM, NMODE).astype(jnp.bfloat16)


def reference(eigvecs, perams, momenta, spins, pair_combs, pair_moms):
    phase = hartley(momenta, jnp.arange(SITES, dtype=jnp.int32))
    blocks = []
    for tslice in range(NSLICE):
        triplet = triplet_slice(eigvecs[tslice], phase).astype(jnp.float32)
        per_comb = []
        for combo in range(COMB):
            p_one = perams[tslice, spins[combo, 0]].astype(jnp.float32)
            p_two = perams[tslice, spins[combo, 1]].astype(jnp.float32)
            p_three = perams[tslice, spins[combo, 2]].astype(jnp.float32)
            first = jnp.einsum('ijpk,mk->ijpm', triplet, p_three).astype(jnp.bfloat16).astype(jnp.float32)
            second = jnp.einsum('mj,ijpk->ipmk', p_two, first).astype(jnp.bfloat16).astype(jnp.float32)
            block = jnp.einsum('mi,ipjk->pmjk', p_one, second).astype(jnp.bfloat16)
            per_comb.append(block)
        blocks.append(jnp.stack(per_comb))
    blocks = jnp.stack(blocks).astype(jnp.float32)

    def one_pair(row):
        comb_pair, mom_pair = row
        left = blocks[:, comb_pair[0], mom_pair[0]]
        right = blocks[:, comb_pair[1], mom_pair[1]]
        return jnp.einsum('tijk,tjil->tkl', left, right) * (1.0 / NMODE)

    return lax.map(one_pair, (pair_combs, pair_moms))
```

```python
import jax
import jax.numpy as jnp
import numpy as np
from jax import lax
from jax.experimental import pallas as pl
from jax.experimental.pallas import tpu as pltpu
from jax.sharding import PartitionSpec as P

LAT = 48
BLK = 8
NBLK = 8
PAIR_BASE = [64 * j * (j + 1) // 2 for j in range(NBLK + 1)]
NPAIR = PAIR_BASE[NBLK]
LANES = 8192
CHUNK = 1024


def roundup(x, m):
    return -(-x // m) * m


ROW_LEN = [PAIR_BASE[j + 1] for j in range(NBLK)]
ROW_OFF = np.concatenate([[0], np.cumsum([roundup(n, 128) for n in ROW_LEN])]).tolist()


def pair_modes():
    first, second = [], []
    for j in range(NBLK):
        width = BLK * (j + 1)
        for i in range(BLK):
            first += list(range(width))
            second += [BLK * j + i] * width
    return np.array([first, second], np.int32)


def segments():
    pieces = []
    for j in range(NBLK):
        done, total = 0, roundup(ROW_LEN[j], 128)
        while done < total:
            at = ROW_OFF[j] + done
            width = min(total - done, CHUNK - at % CHUNK)
            pieces.append((j, done, at // CHUNK, at % CHUNK, width))
            done += width
    return pieces


def nn(a, b):
    return lax.dot_general(a, b, (((1,), (0,)), ((), ())), preferred_element_type=jnp.float32)


def nt(a, b):
    return lax.dot_general(a, b, (((1,), (1,)), ((), ())), preferred_element_type=jnp.float32)


def tn(a, b):
    return lax.dot_general(a, b, (((0,), (0,)), ((), ())), preferred_element_type=jnp.float32)


def bf(x):
    return x.astype(jnp.bfloat16)


VMEM = pl.BlockSpec(memory_space=pltpu.VMEM)
SMEM = pl.BlockSpec(memory_space=pltpu.SMEM)


def split_kernel(x_ref, o_ref):
    peers, _, _, sites = o_ref.shape
    for t in range(x_ref.shape[0]):
        x = x_ref[t].astype(jnp.float32)
        rows = jnp.concatenate([x[m, c : c + 1] for c in range(3) for m in range(x.shape[0])], axis=0)
        for j in range(peers):
            o_ref[j, t] = bf(rows[:, j * sites : (j + 1) * sites])


def split_sites(x, peers):
    nslice, mode_dev, _, site_dev = x.shape
    return pl.pallas_call(
        split_kernel,
        out_shape=jax.ShapeDtypeStruct((peers, nslice, 3 * mode_dev, site_dev // peers), jnp.bfloat16),
        in_specs=[VMEM],
        out_specs=VMEM,
        name="split_sites",
    )(x)


def triplet_kernel(x_ref, phase_ref, o_ref, v_ref, w_ref, d_ref, r_ref):
    t = pl.program_id(0)
    peers, _, rows, sites = x_ref.shape
    mode_dev = rows // 3
    pad = v_ref.shape[2]
    for c in range(3):
        v_ref[c, :, pad - 128 :] = jnp.zeros((v_ref.shape[1], 128), jnp.float32)
        v_ref[c, :, :sites] = jnp.concatenate(
            [x_ref[i, 0].astype(jnp.float32)[c * mode_dev : (c + 1) * mode_dev] for i in range(peers)], axis=0
        )
    for c in range(3):
        v = v_ref[c]
        w = jnp.concatenate(
            [v[BLK * j : BLK * (j + 1)] * phase_ref[p : p + 1] for j in range(NBLK) for p in range(2)], axis=0
        )
        w_ref[c * pad : (c + 1) * pad] = bf(w.T)
    for j in range(NBLK):
        width = BLK * (j + 1)
        for i in range(0, BLK, 2):
            for c in range(3):
                c1, c2 = (c + 1) % 3, (c + 2) % 3
                cross = jnp.concatenate(
                    [
                        v_ref[c1, :width] * v_ref[c2, n : n + 1] - v_ref[c2, :width] * v_ref[c1, n : n + 1]
                        for n in (BLK * j + i, BLK * j + i + 1)
                    ],
                    axis=0,
                )
                d_ref[i * width : (i + 2) * width, c * pad : (c + 1) * pad] = bf(cross)
        part = nn(d_ref[: BLK * width], w_ref[...])
        r_ref[:, PAIR_BASE[j] : PAIR_BASE[j + 1]] = part.T
    for j, pair, chunk, lane, width in segments():
        o_ref[chunk, :, lane : lane + width] = bf(r_ref[2 * BLK * j : 2 * BLK * (j + 1), pair : pair + width])
    used = ROW_OFF[NBLK] % CHUNK
    o_ref[LANES // CHUNK - 1, :, used:] = jnp.zeros((2 * BLK, CHUNK - used), jnp.bfloat16)


def triplet_parts(x, phase):
    peers, nslice, rows, sites = x.shape
    nmode = peers * rows // 3
    pad = phase.shape[1]
    chunks = LANES // CHUNK
    return pl.pallas_call(
        triplet_kernel,
        grid=(nslice,),
        out_shape=jax.ShapeDtypeStruct((nslice * chunks, 2 * BLK, CHUNK), jnp.bfloat16),
        in_specs=[
            pl.BlockSpec((peers, 1, rows, sites), lambda t: (0, t, 0, 0)),
            pl.BlockSpec((2, pad), lambda t: (0, 0)),
        ],
        out_specs=pl.BlockSpec((chunks, 2 * BLK, CHUNK), lambda t: (t, 0, 0)),
        scratch_shapes=[
            pltpu.VMEM((3, nmode, pad), jnp.float32),
            pltpu.VMEM((3 * pad, 2 * nmode), jnp.bfloat16),
            pltpu.VMEM((BLK * nmode, 3 * pad), jnp.bfloat16),
            pltpu.VMEM((2 * nmode, NPAIR), jnp.float32),
        ],
        name="triplet_parts",
    )(x, phase)


def sum_kernel(scale, x_ref, o_ref):
    total = x_ref[0].astype(jnp.float32)
    for i in range(1, x_ref.shape[0]):
        total = total + x_ref[i].astype(jnp.float32)
    total = bf(total * scale)
    for i in range(o_ref.shape[0]):
        o_ref[i] = total


def sum_and_repeat(x, copies, scale):
    def kernel(x_ref, o_ref):
        sum_kernel(scale, x_ref, o_ref)

    return pl.pallas_call(
        kernel,
        out_shape=jax.ShapeDtypeStruct((copies,) + x.shape[1:], jnp.bfloat16),
        in_specs=[VMEM],
        out_specs=VMEM,
        name="sum_and_repeat",
    )(x)


def exchange_kernel(spins_ref, combs_ref, moms_ref, own_ref, tri_ref, per_ref, modes_ref, o_ref, u_ref):
    nmode = per_ref.shape[-1]
    rows_out = o_ref.shape[2]
    spin_a = [spins_ref[combs_ref[0, 0], i] for i in range(3)]
    spin_b = [spins_ref[combs_ref[0, 1], i] for i in range(3)]
    low, mid = modes_ref[0:1], modes_ref[1:2]
    row = lax.broadcasted_iota(jnp.int32, (nmode, NPAIR), 0)
    is_low, is_mid = row == low, row == mid
    one, zero = jnp.float32(1), jnp.float32(0)
    sel_low, sel_mid = bf(jnp.where(is_low, one, zero)), bf(jnp.where(is_mid, one, zero))
    ordered = (low < mid) & (mid < row)
    own_row = lax.broadcasted_iota(jnp.int32, (8, nmode), 0)
    own_col = lax.broadcasted_iota(jnp.int32, (8, nmode), 1)
    own = bf(jnp.where((own_col == own_row + own_ref[0, 0]) & (own_row < rows_out), one, zero))

    def slices(t, carry):
        for j, pair, chunk, lane, width in segments():
            both = tri_ref[t * (LANES // CHUNK) + chunk, :, lane : lane + width].astype(jnp.float32)
            for side in range(2):
                picked = jnp.where(moms_ref[0, side] == 0, both[:BLK], both[BLK:])
                u_ref[side, BLK * j : BLK * (j + 1), pair : pair + width] = picked
        tri_a = jnp.where(ordered, u_ref[0], zero)
        tri_b = jnp.where(ordered, u_ref[1], zero)
        p1a, p2a, p3a = [per_ref[t, s] for s in spin_a]
        p1b, p2b, p3b = [per_ref[t, s] for s in spin_b]
        q = bf(nn(own, p3a))
        q_low, q_mid = nn(q, sel_low), nn(q, sel_mid)
        pairs = nn(q, bf(tri_a))
        to_mid = jnp.concatenate(
            [bf(jnp.where(is_low, pairs[k : k + 1], -tri_a * q_low[k : k + 1])) for k in range(rows_out)], axis=0
        )
        to_low = jnp.concatenate([bf(tri_a * q_mid[k : k + 1]) for k in range(rows_out)], axis=0)
        half = nt(to_mid, sel_mid) + nt(to_low, sel_low)
        cut = lambda x, k: x[k * nmode : (k + 1) * nmode]
        anti = [cut(half, k) - cut(half, k).T for k in range(rows_out)]
        right = bf(nt(bf(jnp.concatenate(anti, axis=0)), p2a))
        block = jnp.concatenate([bf(nn(p1a, cut(right, k))) for k in range(rows_out)], axis=0)
        turned = bf(nn(block, p1b))
        back = [tn(p2b, cut(turned, k)) for k in range(rows_out)]
        weight = bf(jnp.concatenate([x.T - x for x in back], axis=0))
        at_low, at_mid = nn(weight, sel_low), nn(weight, sel_mid)
        fill = jnp.zeros((8 - rows_out, NPAIR), jnp.float32)

        def stack(f):
            return bf(jnp.concatenate([jnp.sum(f(k), axis=0, keepdims=True) for k in range(rows_out)] + [fill], axis=0))

        on_high = stack(lambda k: jnp.where(is_mid, cut(at_low, k), zero))
        on_mid = stack(lambda k: cut(at_low, k) * tri_b)
        on_low = stack(lambda k: cut(at_mid, k) * tri_b)
        ends = nt(on_mid, sel_mid) - nt(on_low, sel_low) - nt(on_high, bf(tri_b))
        head = bf(ends)
        tail = bf(ends - head.astype(jnp.float32))
        o_ref[0, t] = ((nt(head, p3b) + nt(tail, p3b)) * (1.0 / nmode))[:rows_out]
        return carry

    lax.fori_loop(0, o_ref.shape[1], slices, 0)


def exchange_rows(spins, pair_combs, pair_moms, own, triplets, perams, rows_out):
    nslice, _, nmode, _ = perams.shape
    return pl.pallas_call(
        exchange_kernel,
        out_shape=jax.ShapeDtypeStruct((1, nslice, rows_out, nmode), jnp.float32),
        in_specs=[SMEM, SMEM, SMEM, SMEM, VMEM, VMEM, VMEM],
        out_specs=VMEM,
        scratch_shapes=[pltpu.VMEM((2, nmode, NPAIR), jnp.float32)],
        name="exchange_rows",
    )(spins, pair_combs, pair_moms, own, triplets, perams, jnp.asarray(pair_modes()))


def hartley(momenta, glob):
    coord_x = glob // (LAT * LAT)
    coord_y = glob // LAT % LAT
    coord_z = glob % LAT
    wave = (
        momenta[:, 0:1] * coord_x[None]
        + momenta[:, 1:2] * coord_y[None]
        + momenta[:, 2:3] * coord_z[None]
    ) % LAT
    theta = wave.astype(jnp.float32) * (2.0 * jnp.pi / LAT)
    return jnp.cos(theta) + jnp.sin(theta)


def swap(x, axis):
    return lax.all_to_all(x, axis, split_axis=0, concat_axis=0)


def body(eigvecs, perams, momenta, spins, pair_combs, pair_moms):
    nslice, mode_dev, _, site_dev = eigvecs.shape
    peers = lax.axis_size("mode")
    sites = site_dev // peers
    mode_id = lax.axis_index("mode")
    start = lax.axis_index("site") * site_dev + mode_id * sites
    phase = hartley(momenta, start + jnp.arange(roundup(sites, 128), dtype=jnp.int32))
    vectors = swap(split_sites(eigvecs, peers), "mode")
    parts = swap(triplet_parts(vectors, phase), "mode")
    parts = swap(sum_and_repeat(parts, lax.axis_size("site"), 1.0), "site")
    triplets = swap(sum_and_repeat(parts, peers, float(LAT) ** (-1.5)), "mode")
    own = (mode_id * mode_dev).reshape(1, 1).astype(jnp.int32)
    return exchange_rows(spins, pair_combs, pair_moms, own, triplets, perams, mode_dev)


def solution(mesh):
    placed = (P(None, "mode", None, "site"), P(), P(), P(), P("site", None), P("site", None))
    return jax.shard_map(
        body, mesh=mesh, in_specs=placed, out_specs=P("site", None, "mode", None), check_vma=False
    )
```

```python
import jax
import jax.numpy as jnp
import numpy as np
from jax import lax
from jax.experimental import pallas as pl
from jax.experimental.pallas import tpu as pltpu
from jax.sharding import Mesh
from jax.sharding import PartitionSpec as P

LAT = 48
BLK = 8
NBLK = 8
PAIR_BASE = [64 * j * (j + 1) // 2 for j in range(NBLK + 1)]
NPAIR = PAIR_BASE[NBLK]
LANES = 8192
CHUNK = 512


def roundup(x, m):
    return -(-x // m) * m


ROW_LEN = [PAIR_BASE[j + 1] for j in range(NBLK)]
ROW_OFF = np.concatenate([[0], np.cumsum([roundup(n, 128) for n in ROW_LEN])]).tolist()


def pair_modes():
    first, second = [], []
    for j in range(NBLK):
        width = BLK * (j + 1)
        for i in range(BLK):
            first += list(range(width))
            second += [BLK * j + i] * width
    return np.array([first, second], np.int32)


def segments():
    pieces = []
    for j in range(NBLK):
        done, total = 0, roundup(ROW_LEN[j], 128)
        while done < total:
            at = ROW_OFF[j] + done
            width = min(total - done, CHUNK - at % CHUNK)
            pieces.append((j, done, at // CHUNK, at % CHUNK, width))
            done += width
    return pieces


def nn(a, b):
    return lax.dot_general(a, b, (((1,), (0,)), ((), ())), preferred_element_type=jnp.float32)


def nt(a, b):
    return lax.dot_general(a, b, (((1,), (1,)), ((), ())), preferred_element_type=jnp.float32)


def tn(a, b):
    return lax.dot_general(a, b, (((0,), (0,)), ((), ())), preferred_element_type=jnp.float32)


def bf(x):
    return x.astype(jnp.bfloat16)


VMEM = pl.BlockSpec(memory_space=pltpu.VMEM)
SMEM = pl.BlockSpec(memory_space=pltpu.SMEM)

MODE = ("x_hi", "y", "core")
SITE = ("z", "x_lo")
PLANE = ("x_hi", "y", "core", "x_lo")


def on_chip(x):
    return pltpu.with_memory_space_constraint(x, pltpu.VMEM)


def split_kernel(x_ref, o_ref):
    peers, _, sites = o_ref.shape
    nslice, ncolor, mode_dev, _ = x_ref.shape
    x = jnp.concatenate([x_ref[t, c].astype(jnp.float32) for t in range(nslice) for c in range(ncolor)], axis=0)
    for j in range(peers):
        o_ref[j] = bf(x[:, j * sites : (j + 1) * sites])


def split_sites(x, peers):
    nslice, ncolor, mode_dev, site_dev = x.shape
    return pl.pallas_call(
        split_kernel,
        out_shape=pltpu.VMEM((peers, nslice * ncolor * mode_dev, site_dev // peers), jnp.bfloat16),
        in_specs=[VMEM],
        out_specs=VMEM,
        name="split_sites",
    )(x)


def triplet_kernel(x_ref, phase_ref, o_ref, v_ref, w_ref, d_ref, r_ref):
    nslice, ncolor, nmode, pad = v_ref.shape
    peers, rows, sites = x_ref.shape
    mode_dev = nmode // peers
    x = [x_ref[i].astype(jnp.float32) for i in range(peers)]
    for t in range(nslice):
        for c in range(ncolor):
            at = (t * ncolor + c) * mode_dev
            v_ref[t, c, :, pad - 128 :] = jnp.zeros((nmode, 128), jnp.float32)
            v_ref[t, c, :, :sites] = jnp.concatenate([y[at : at + mode_dev] for y in x], axis=0)

    def one_slice(t, carry):
        for c in range(ncolor):
            v = v_ref[t, c]
            w = jnp.concatenate(
                [v[BLK * j : BLK * (j + 1)] * phase_ref[p : p + 1] for j in range(NBLK) for p in range(2)], axis=0
            )
            w_ref[c * pad : (c + 1) * pad] = bf(w.T)
        for j in range(NBLK):
            width = BLK * (j + 1)
            for i in range(0, BLK, 2):
                for c in range(ncolor):
                    c1, c2 = (c + 1) % ncolor, (c + 2) % ncolor
                    cross = jnp.concatenate(
                        [
                            v_ref[t, c1, :width] * v_ref[t, c2, n : n + 1]
                            - v_ref[t, c2, :width] * v_ref[t, c1, n : n + 1]
                            for n in (BLK * j + i, BLK * j + i + 1)
                        ],
                        axis=0,
                    )
                    d_ref[i * width : (i + 2) * width, c * pad : (c + 1) * pad] = bf(cross)
            part = nn(d_ref[: BLK * width], w_ref[...])
            r_ref[:, PAIR_BASE[j] : PAIR_BASE[j + 1]] = part.T
        first = t * (LANES // CHUNK)
        for j, pair, chunk, lane, width in segments():
            o_ref[first + chunk, :, lane : lane + width] = bf(
                r_ref[2 * BLK * j : 2 * BLK * (j + 1), pair : pair + width]
            )
        used = ROW_OFF[NBLK] % CHUNK
        o_ref[first + LANES // CHUNK - 1, :, used:] = jnp.zeros((2 * BLK, CHUNK - used), jnp.bfloat16)
        return carry

    lax.fori_loop(0, nslice, one_slice, 0)


def triplet_parts(x, phase, nslice):
    peers, rows, sites = x.shape
    mode_dev = rows // (3 * nslice)
    nmode = peers * mode_dev
    pad = phase.shape[1]
    return pl.pallas_call(
        triplet_kernel,
        out_shape=pltpu.VMEM((nslice * LANES // CHUNK, 2 * BLK, CHUNK), jnp.bfloat16),
        in_specs=[VMEM, VMEM],
        out_specs=VMEM,
        scratch_shapes=[
            pltpu.VMEM((nslice, 3, nmode, pad), jnp.float32),
            pltpu.VMEM((3 * pad, 2 * nmode), jnp.bfloat16),
            pltpu.VMEM((BLK * nmode, 3 * pad), jnp.bfloat16),
            pltpu.VMEM((2 * nmode, NPAIR), jnp.float32),
        ],
        name="triplet_parts",
    )(on_chip(x), on_chip(phase))


def sum_kernel(scale, x_ref, o_ref):
    total = x_ref[0].astype(jnp.float32)
    for i in range(1, x_ref.shape[0]):
        total = total + x_ref[i].astype(jnp.float32)
    total = bf(total * scale)
    for i in range(o_ref.shape[0]):
        o_ref[i] = total


def sum_and_repeat(x, copies, scale):
    def kernel(x_ref, o_ref):
        sum_kernel(scale, x_ref, o_ref)

    return pl.pallas_call(
        kernel,
        out_shape=pltpu.VMEM((copies,) + x.shape[1:], jnp.bfloat16),
        in_specs=[VMEM],
        out_specs=VMEM,
        name="sum_and_repeat",
    )(on_chip(x))


def exchange_kernel(spins_ref, combs_ref, moms_ref, own_ref, tri_ref, per_ref, modes_ref, o_ref, u_ref):
    nmode = per_ref.shape[-1]
    slices, rows_out = range(o_ref.shape[1]), o_ref.shape[2]
    spin_a = [spins_ref[combs_ref[0, 0], i] for i in range(3)]
    spin_b = [spins_ref[combs_ref[0, 1], i] for i in range(3)]
    low, mid = modes_ref[0:1], modes_ref[1:2]
    row = lax.broadcasted_iota(jnp.int32, (nmode, NPAIR), 0)
    is_low, is_mid = row == low, row == mid
    one, zero = jnp.float32(1), jnp.float32(0)
    sel_low, sel_mid = bf(jnp.where(is_low, one, zero)), bf(jnp.where(is_mid, one, zero))
    ordered = (low < mid) & (mid < row)
    own_row = lax.broadcasted_iota(jnp.int32, (8, nmode), 0)
    own_col = lax.broadcasted_iota(jnp.int32, (8, nmode), 1)
    own = bf(jnp.where((own_col == own_row + own_ref[0, 0]) & (own_row < rows_out), one, zero))
    stack = lambda xs: jnp.concatenate(list(xs), axis=0)
    cut = lambda x, i: x[i * nmode : (i + 1) * nmode]
    each = [(t, k, t * rows_out + k) for t in slices for k in range(rows_out)]
    for t in slices:
        for j, pair, chunk, lane, width in segments():
            both = tri_ref[t * (LANES // CHUNK) + chunk, :, lane : lane + width].astype(jnp.float32)
            for side in range(2):
                picked = jnp.where(moms_ref[0, side] == 0, both[:BLK], both[BLK:])
                u_ref[t, side, BLK * j : BLK * (j + 1), pair : pair + width] = picked
    tri_a = [jnp.where(ordered, u_ref[t, 0], zero) for t in slices]
    tri_b = [jnp.where(ordered, u_ref[t, 1], zero) for t in slices]
    mats_a = [[per_ref[t, s] for s in spin_a] for t in slices]
    mats_b = [[per_ref[t, s] for s in spin_b] for t in slices]
    q = bf(stack(nn(own, mats_a[t][2]) for t in slices))
    q_low, q_mid = nn(q, sel_low), nn(q, sel_mid)
    pairs = [nn(q[8 * t : 8 * t + 8], bf(tri_a[t])) for t in slices]
    line = lambda x, t, k: x[8 * t + k : 8 * t + k + 1]
    to_mid = stack(bf(jnp.where(is_low, pairs[t][k : k + 1], -tri_a[t] * line(q_low, t, k))) for t, k, _ in each)
    to_low = stack(bf(tri_a[t] * line(q_mid, t, k)) for t, k, _ in each)
    half = nt(to_mid, sel_mid) + nt(to_low, sel_low)
    anti = [bf(cut(half, i) - cut(half, i).T) for _, _, i in each]
    size = rows_out * nmode
    right = [bf(nt(stack(anti[t * rows_out : (t + 1) * rows_out]), mats_a[t][1])) for t in slices]
    block = [stack(bf(nn(mats_a[t][0], cut(right[t], k))) for k in range(rows_out)) for t in slices]
    turned = [bf(nn(block[t], mats_b[t][0])) for t in slices]
    back = [tn(mats_b[t][1], cut(turned[t], k)) for t, k, _ in each]
    weight = bf(stack(x.T - x for x in back))
    at_low, at_mid = nn(weight, sel_low), nn(weight, sel_mid)
    fill = [jnp.zeros((8 - rows_out, NPAIR), jnp.float32)]

    def summed(f):
        return [
            bf(stack([jnp.sum(f(t, t * rows_out + k), axis=0, keepdims=True) for k in range(rows_out)] + fill))
            for t in slices
        ]

    on_high = summed(lambda t, i: jnp.where(is_mid, cut(at_low, i), zero))
    on_mid = stack(summed(lambda t, i: cut(at_low, i) * tri_b[t]))
    on_low = stack(summed(lambda t, i: cut(at_mid, i) * tri_b[t]))
    ends = nt(on_mid, sel_mid) - nt(on_low, sel_low) - stack(nt(on_high[t], bf(tri_b[t])) for t in slices)
    head = bf(ends)
    tail = bf(ends - head.astype(jnp.float32))
    for t in slices:
        mat, own_rows = mats_b[t][2], slice(8 * t, 8 * t + 8)
        o_ref[0, t] = ((nt(head[own_rows], mat) + nt(tail[own_rows], mat)) * (1.0 / nmode))[:rows_out]


def exchange_rows(spins, pair_combs, pair_moms, own, triplets, perams, rows_out):
    nslice, _, nmode, _ = perams.shape
    return pl.pallas_call(
        exchange_kernel,
        out_shape=jax.ShapeDtypeStruct((1, nslice, rows_out, nmode), jnp.float32),
        in_specs=[SMEM, SMEM, SMEM, SMEM, VMEM, VMEM, VMEM],
        out_specs=VMEM,
        scratch_shapes=[pltpu.VMEM((nslice, 2, nmode, NPAIR), jnp.float32)],
        name="exchange_rows",
    )(spins, pair_combs, pair_moms, own, on_chip(triplets), on_chip(perams), jnp.asarray(pair_modes()))


def hartley(momenta, glob):
    coord_x = glob // (LAT * LAT)
    coord_y = glob // LAT % LAT
    coord_z = glob % LAT
    wave = (
        momenta[:, 0:1] * coord_x[None]
        + momenta[:, 1:2] * coord_y[None]
        + momenta[:, 2:3] * coord_z[None]
    ) % LAT
    theta = wave.astype(jnp.float32) * (2.0 * jnp.pi / LAT)
    return jnp.cos(theta) + jnp.sin(theta)


def swap(x, axis):
    return lax.all_to_all(x, axis, split_axis=0, concat_axis=0)


def body(eigvecs, perams, momenta, spins, pair_combs, pair_moms):
    nslice, mode_dev, _, site_dev = eigvecs.shape
    peers = lax.axis_size(MODE)
    sites = site_dev // peers
    mode_id = lax.axis_index(MODE)
    start = lax.axis_index(SITE) * site_dev + mode_id * sites
    phase = hartley(momenta, start + jnp.arange(roundup(sites, 128), dtype=jnp.int32))
    vectors = swap(split_sites(eigvecs.transpose(0, 2, 1, 3), peers), MODE)
    parts = swap(triplet_parts(vectors, phase, nslice), PLANE)
    parts = swap(sum_and_repeat(parts, lax.axis_size("z"), 1.0), "z")
    triplets = swap(sum_and_repeat(parts, lax.axis_size(PLANE), float(LAT) ** (-1.5)), PLANE)
    own = (mode_id * mode_dev).reshape(1, 1).astype(jnp.int32)
    return exchange_rows(spins, pair_combs, pair_moms, own, triplets, perams, mode_dev)


def solution(mesh):
    fine = Mesh(mesh.devices.reshape(2, 4, 2, 8, 2), MODE + SITE)
    placed = (P(None, MODE, None, SITE), P(), P(), P(), P(SITE, None), P(SITE, None))
    return jax.shard_map(
        body, mesh=fine, in_specs=placed, out_specs=P(SITE, None, MODE, None), check_vma=False
    )
```
